32 devices in a mesh: rows: 16 (over z, x, core), dp: 2 (over y).
Axes of the slice: x: 2, y: 2, z: 4, core: 2. Of those that a mesh axis runs over, the one named last changes fastest.
Arguments:
- query_act: bfloat16 [128, 64, 128], P(('dp', 'rows')), parts along dimension 0, may hold values from -2.09375 to 2.09375
- key_act: bfloat16 [128, 64, 128], P(('dp', 'rows')), parts along dimension 0, may hold values from -2.09375 to 2.09375
- value_act: bfloat16 [128, 64, 128], P(('dp', 'rows')), parts along dimension 0, may hold values from -4 to 4
- attn_out: bfloat16 [128, 64, 128], P(('dp', 'rows')), parts along dimension 0, may hold values from -4 to 4
- grad_out: bfloat16 [128, 64, 128], P(('dp', 'rows')), parts along dimension 0, may hold values from -4 to 4
- pair_bias: bfloat16 [4, 128, 64], P(None, ('dp', 'rows')), parts along dimension 1, may hold values from -3 to 3
- log_norm: float32 [128, 4, 64], P(('dp', 'rows')), parts along dimension 0, may hold values from 6.8 to 8
- back_weight: bfloat16 [384, 128], replicated, may hold values from -2 to 2
Outputs:
- column_grad: bfloat16 [64, 128, 128], P('rows', 'dp'), parts along dimension 1
- bias_grad: float32 [4, 128, 64], P(None, ('dp', 'rows')), parts along dimension 1
The draws below stay inside these ranges and needn't reach their ends.
There are 2 independent parts, one for each index of `dp`. The reference program is written for one: setup_inputs(seed, part) draws one part's arguments, and reference() takes and returns one part's arrays. A program takes and returns all parts, laid end to end along the dimension named above; an argument that names none is the same for every part. Nothing has to cross between parts.
All inputs are finite; a program needn't handle non-finite values.
Results may differ from the reference program's by a relative error of at most 0.008.
Values may be sent and summed in bfloat16 or wider, within the bound.
A program may use at most 64 MiB of HBM per device.

```python
import jax
import jax.numpy as jnp
from jax import lax

C = 128
HEADS = 4
HD = 128
N = 64


def raised(array, own_key, source, target, parts, factor):
    def block_of(position):
        return (jnp.arange(array.shape[position]) // (array.shape[position] // parts)).reshape((-1,) + (1,) * (array.ndim - 1 - position))

    first = jax.random.permutation(own_key, parts)[block_of(target)]
    far = (block_of(target) + parts // 2) % parts
    return jnp.where((block_of(source) == first) | (block_of(source) == far), factor * array, array)


def block_levels(own_key, dims, cuts, low, high):
    def one(axis_at, shards_of):
        steps = jax.random.uniform(jax.random.fold_in(jax.random.fold_in(own_key, 6), axis_at), (shards_of,), jnp.float32, low / len(cuts), high / len(cuts))
        return jnp.repeat(jnp.exp(steps), dims[axis_at] // shards_of).reshape((-1,) + (1,) * (len(dims) - axis_at - 1))

    loudness = one(*cuts[0])
    for cut in cuts[1:]:
        loudness = loudness * one(*cut)
    return loudness


def scatter_about(key, dims, width, most, cuts=(), dtype=jnp.bfloat16):
    level = block_levels(key, dims, cuts, -0.22, 0.18) if cuts else 1.0
    result = jax.random.normal(key, dims, jnp.float32) * width * level
    return jnp.minimum(jnp.maximum(result, -most), most).astype(dtype)


def heavy_noise(stream_key, dims, spread, most, cuts, heavy, kind=jnp.bfloat16):
    drawn = spread * jax.random.normal(stream_key, dims, jnp.float32)
    if cuts:
        drawn = drawn * block_levels(stream_key, dims, cuts, -0.22, 0.18)
    return jnp.clip(raised(drawn, jax.random.fold_in(stream_key, 3), *heavy), -most, most).astype(kind)


def setup_inputs(seed: int = 0, part: int = 0) -> dict:
    seeds = jax.random.split(jax.random.key(seed), 9)
    own_keys = jax.random.split(jax.random.fold_in(seeds[8], part), 9)
    query_act = scatter_about(own_keys[0], (N, N, HD), 0.7, 2.09375, ((0, 16),))
    key_act = scatter_about(own_keys[1], (N, N, HD), 0.7, 2.09375, ((0, 16),))
    value_act = scatter_about(own_keys[2], (N, N, HD), 1.0, 4.0, ((0, 16),))
    attn_out = scatter_about(own_keys[3], (N, N, HD), 1.0, 4.0, ((0, 16),))
    grad_out = heavy_noise(own_keys[4], (N, N, HD), 1.0, 4.0, ((0, 16),), (0, 1, 16, 2.0))
    pair_bias = scatter_about(own_keys[5], (HEADS, N, N), 1.0, 3.0, ((1, 16),))
    log_norm = jnp.clip(6.8 + 1.1999998 * jax.random.uniform(own_keys[6], (N, HEADS, N), jnp.float32) ** block_levels(own_keys[6], (N, HEADS, N), ((0, 16),), -0.2, 0.2), 6.8, 8.0)
    back_weight = scatter_about(seeds[7], (3 * HD, C), 0.5, 2.0)
    return {"query_act": query_act, "key_act": key_act, "value_act": value_act, "attn_out": attn_out, "grad_out": grad_out, "pair_bias": pair_bias, "log_norm": log_norm, "back_weight": back_weight}


def reference(query_act, key_act, value_act, attn_out, grad_out, pair_bias, log_norm, back_weight):
    length = query_act.shape[1]
    head_count = pair_bias.shape[0]
    head_size = query_act.shape[2] // head_count
    softmax_scale = head_size ** -0.5
    bias_full = pair_bias.astype(jnp.float32)

    def single_row(running, inputs):
        query_row, key_row, value_row, out_row, grad_row, norm_row = inputs
        query_h = query_row.astype(jnp.float32).reshape(length, head_count, head_size)
        key_h = key_row.astype(jnp.float32).reshape(length, head_count, head_size)
        value_h = value_row.astype(jnp.float32).reshape(length, head_count, head_size)
        out_h = out_row.astype(jnp.float32).reshape(length, head_count, head_size)
        grad_h = grad_row.astype(jnp.float32).reshape(length, head_count, head_size)
        scores = jnp.einsum("jhd,khd->hjk", query_h, key_h) * softmax_scale + bias_full
        probs = jnp.exp(scores - norm_row[:, :, None])
        probs_low = lax.optimization_barrier(probs.astype(jnp.bfloat16)).astype(jnp.float32)
        grad_value = jnp.einsum("hjk,jhd->khd", probs_low, grad_h)
        grad_prob = jnp.einsum("jhd,khd->hjk", grad_h, value_h)
        row_delta = jnp.einsum("jhd,jhd->hj", grad_h, out_h)
        grad_score = probs * (grad_prob - row_delta[:, :, None])
        score_low = lax.optimization_barrier(grad_score.astype(jnp.bfloat16)).astype(jnp.float32)
        grad_query = jnp.einsum("hjk,khd->jhd", score_low, key_h) * softmax_scale
        grad_key = jnp.einsum("hjk,jhd->khd", score_low, query_h) * softmax_scale
        joined = jnp.concatenate([grad_query.reshape(length, -1), grad_key.reshape(length, -1), grad_value.reshape(length, -1)], axis=1).astype(jnp.bfloat16)
        pair_row = jnp.dot(joined, back_weight, preferred_element_type=jnp.float32).astype(jnp.bfloat16)
        return running + grad_score, pair_row

    initial = jnp.zeros(pair_bias.shape, jnp.float32)
    bias_grad, pair_rows = lax.scan(single_row, initial, (query_act, key_act, value_act, attn_out, grad_out, log_norm))
    return jnp.transpose(pair_rows, (1, 0, 2)), bias_grad
```

```python
import functools

import jax
import jax.numpy as jnp
from jax import lax
from jax.experimental import pallas as pl
from jax.experimental.pallas import tpu as pltpu
from jax.sharding import PartitionSpec as P

MESH = pl.DeviceIdType.MESH
BLOCK = 64
UNROLL = 16
F32 = jnp.float32
BF16 = jnp.bfloat16


def repeat(count, body):
    if count <= UNROLL:
        for step in range(count):
            body(step)
    else:
        lax.fori_loop(0, count, lambda step, carry: (body(step), carry)[1], 0)


def block_of(length):
    for width in range(min(length, BLOCK), 0, -1):
        if length % width == 0:
            return width


def nt(left, right):
    return lax.dot_general(left, right, (((1,), (1,)), ((), ())), preferred_element_type=F32)


def tn(left, right):
    return lax.dot_general(left, right, (((0,), (0,)), ((), ())), preferred_element_type=F32)


def nn(left, right):
    return jnp.dot(left, right, preferred_element_type=F32)


def kernel(
    n,
    query_hbm, key_hbm, value_hbm, out_hbm, grad_hbm, bias_hbm, norm_hbm, weight_hbm,
    pair_out, bias_out,
    query, key, value, attn, grad, bias, norm, weight,
    factor_own, factor, part, part_in, probs_free, score_free,
    key_wide, norm_rows, joined, pair_send,
    in_sem, factor_sem, part_sem, pair_sem, own_sem,
):
    me = lax.axis_index("rows")
    rows, length, width = query.shape
    heads = bias.shape[0]
    own = bias.shape[1]
    size = width // heads
    scale = size ** (-0.5)
    block = block_of(length)
    chunks = length // block
    owners = block // own
    wide = heads * length

    loads = []
    for at, (source, target) in enumerate(
        (
            (bias_hbm, bias), (query_hbm, query), (key_hbm, key), (norm_hbm, norm),
            (grad_hbm, grad), (out_hbm, attn), (value_hbm, value), (weight_hbm, weight),
        )
    ):
        load = pltpu.make_async_copy(source, target, in_sem.at[at])
        load.start()
        loads.append(load)

    def peer(step):
        return lax.rem(me + step + 1, n)

    barrier = pltpu.get_barrier_semaphore()
    repeat(
        n - 1,
        lambda step: pl.semaphore_signal(
            barrier, inc=1, device_id={"rows": peer(step)}, device_id_type=MESH
        ),
    )

    loads[0].wait()
    own_factor = jnp.exp(
        jnp.concatenate([bias[h].astype(F32) for h in range(heads)], axis=1)
    )
    factor_own[...] = own_factor
    for load in loads[1:7]:
        load.wait()

    head_mask = (
        lax.broadcasted_iota(jnp.int32, (wide, width), 0) // length
        == lax.broadcasted_iota(jnp.int32, (wide, width), 1) // size
    )
    spread = (
        lax.broadcasted_iota(jnp.int32, (2 * width, wide), 0) % width // size
        == lax.broadcasted_iota(jnp.int32, (2 * width, wide), 1) // length
    ).astype(F32).astype(BF16)
    norm_spread = (
        lax.broadcasted_iota(jnp.int32, (3 * heads, wide), 0) % heads
        == lax.broadcasted_iota(jnp.int32, (3 * heads, wide), 1) // length
    ).astype(F32).astype(BF16)

    def widen(array):
        zero = jnp.zeros((wide, width), BF16)
        return jnp.where(head_mask, jnp.concatenate([array] * heads, axis=0), zero)

    def norm_terms(array):
        first = array.astype(BF16).astype(F32)
        second = (array - first).astype(BF16).astype(F32)
        third = array - first - second
        return jnp.concatenate([first, second, third], axis=0).astype(BF16)

    for i in range(rows):
        key_wide[i] = widen(key[i])
        if chunks > 1:
            same = (
                lax.broadcasted_iota(jnp.int32, (3 * heads, 3 * heads), 0)
                == lax.broadcasted_iota(jnp.int32, (3 * heads, 3 * heads), 1)
            ).astype(F32).astype(BF16)
            norm_rows[i] = tn(norm_terms(norm[i]), same)

    def free_part(chunk):
        at = chunk * block if chunks == 1 else pl.multiple_of(chunk * block, block)
        total = None
        for i in range(rows):
            span = pl.ds(at, block)
            grad_i = grad[i, span, :]
            product = grad_i.astype(F32) * attn[i, span, :].astype(F32)
            high = product.astype(BF16)
            low = (product - high.astype(F32)).astype(BF16)
            delta = nn(jnp.concatenate([high, low], axis=1), spread)
            if chunks == 1:
                norm_wide = tn(norm_terms(norm[i]), norm_spread)
            else:
                norm_wide = nn(norm_rows[i, span, :].astype(BF16), norm_spread)
            scores = nt(query[i, span, :], key_wide[i]) * scale
            probs = jnp.exp(scores - norm_wide)
            score = probs * (nt(grad_i, widen(value[i])) - delta)
            probs_free[i, span, :] = probs
            score_free[i, span, :] = score
            total = score if total is None else total + score
        part[pl.ds(chunk * owners, owners)] = total.reshape(owners, own, wide)

    repeat(chunks, free_part) if chunks == 1 else lax.fori_loop(
        0, chunks, lambda c, carry: (free_part(c), carry)[1], 0
    )
    factor[me] = own_factor

    pl.semaphore_wait(barrier, n - 1)

    def send_factor(step):
        pltpu.make_async_remote_copy(
            src_ref=factor_own, dst_ref=factor.at[me],
            send_sem=factor_sem.at[0], recv_sem=factor_sem.at[1],
            device_id={"rows": peer(step)}, device_id_type=MESH,
        ).start()

    def send_part(step):
        other = peer(step)
        pltpu.make_async_remote_copy(
            src_ref=part.at[other], dst_ref=part_in.at[me],
            send_sem=part_sem.at[0], recv_sem=part_sem.at[1],
            device_id={"rows": other}, device_id_type=MESH,
        ).start()

    def send_pair(step):
        other = peer(step)
        pltpu.make_async_remote_copy(
            src_ref=pair_send.at[:, other], dst_ref=pair_out.at[me],
            send_sem=pair_sem.at[0], recv_sem=pair_sem.at[1],
            device_id={"rows": other}, device_id_type=MESH,
        ).start()

    def all_of(ref, sem):
        view = ref.at[pl.ds(0, n - 1)]
        pltpu.make_async_copy(view, view, sem).wait()

    repeat(n - 1, send_factor)
    part_in[me] = part[me]
    loads[7].wait()
    all_of(factor, factor_sem.at[1])
    repeat(n - 1, send_part)

    def fold(array):
        folded = None
        for h in range(heads):
            keep = lax.broadcasted_iota(jnp.int32, (length, width), 1) // size == h
            piece = jnp.where(keep, array[h * length : (h + 1) * length], 0.0)
            folded = piece if folded is None else folded + piece
        return folded

    if chunks == 1:
        factor_all = factor[...].reshape(length, wide)
        pieces = []
        for i in range(rows):
            probs_low = (probs_free[i] * factor_all).astype(BF16)
            score_low = (score_free[i] * factor_all).astype(BF16)
            grad_query = nn(score_low, key_wide[i]) * scale
            grad_key = fold(tn(score_low, query[i])) * scale
            grad_value = fold(tn(probs_low, grad[i]))
            pieces.append(
                jnp.concatenate([grad_query, grad_key, grad_value], axis=1).astype(BF16)
            )
        for i in range(rows):
            pair = nn(pieces[i], weight[...]).astype(BF16)
            pair_send[i] = pair.reshape(n, own, weight.shape[1])
    else:
        for i in range(rows):
            joined[...] = jnp.zeros_like(joined)

            def advance(chunk, carry):
                span = pl.ds(pl.multiple_of(chunk * block, block), block)
                factor_part = factor[pl.ds(chunk * owners, owners)].reshape(block, wide)
                probs_low = (probs_free[i, span, :] * factor_part).astype(BF16)
                score_low = (score_free[i, span, :] * factor_part).astype(BF16)
                joined[0, span, :] = nn(score_low, key_wide[i]) * scale
                joined[1] += fold(tn(score_low, query[i, span, :]))
                joined[2] += fold(tn(probs_low, grad[i, span, :]))
                return carry

            lax.fori_loop(0, chunks, advance, 0)
            whole = jnp.concatenate(
                [joined[0], joined[1] * scale, joined[2]], axis=1
            ).astype(BF16)
            pair = nn(whole, weight[...]).astype(BF16)
            pair_send[i] = pair.reshape(n, own, weight.shape[1])

    keep_own = pltpu.make_async_copy(pair_send.at[:, me], pair_out.at[me], own_sem)
    keep_own.start()
    repeat(n - 1, send_pair)

    all_of(part_in, part_sem.at[1])
    total = jnp.sum(part_in[...], axis=0) * factor_own[...]
    for h in range(heads):
        bias_out[h] = total[:, h * length : (h + 1) * length]

    keep_own.wait()
    all_of(factor, factor_sem.at[0])
    all_of(part_in, part_sem.at[0])
    all_of(pair_out, pair_sem.at[0])
    all_of(pair_out, pair_sem.at[1])


def local(n, query_act, key_act, value_act, attn_out, grad_out, pair_bias, log_norm, back_weight):
    rows, length, width = query_act.shape
    heads, own, _ = pair_bias.shape
    channels = back_weight.shape[1]
    wide = heads * length
    chunked = length // block_of(length) > 1
    act = pltpu.VMEM((rows, length, width), BF16)
    anywhere = pl.BlockSpec(memory_space=pl.ANY)
    pairs, bias_grad = pl.pallas_call(
        functools.partial(kernel, n),
        out_shape=(
            jax.ShapeDtypeStruct((n, rows, own, channels), BF16),
            jax.ShapeDtypeStruct((heads, own, length), F32),
        ),
        in_specs=[anywhere] * 8,
        out_specs=(anywhere, pl.BlockSpec(memory_space=pltpu.VMEM)),
        scratch_shapes=[
            act, act, act, act, act,
            pltpu.VMEM(pair_bias.shape, BF16),
            pltpu.VMEM(log_norm.shape, F32),
            pltpu.VMEM(back_weight.shape, BF16),
            pltpu.VMEM((own, wide), F32),
            pltpu.VMEM((n, own, wide), F32),
            pltpu.VMEM((n, own, wide), F32),
            pltpu.VMEM((n, own, wide), F32),
            pltpu.VMEM((rows, length, wide), F32),
            pltpu.VMEM((rows, length, wide), F32),
            pltpu.VMEM((rows, wide, width), BF16),
            pltpu.VMEM((rows, length, 3 * heads) if chunked else (rows, 8, 3 * heads), F32),
            pltpu.VMEM((3, length, width) if chunked else (3, 8, 128), F32),
            pltpu.VMEM((rows, n, own, channels), BF16),
            pltpu.SemaphoreType.DMA((8,)),
            pltpu.SemaphoreType.DMA((2,)),
            pltpu.SemaphoreType.DMA((2,)),
            pltpu.SemaphoreType.DMA((2,)),
            pltpu.SemaphoreType.DMA,
        ],
        compiler_params=pltpu.CompilerParams(
            collective_id=0, has_side_effects=True, vmem_limit_bytes=67043328 - (2 << 20)
        ),
    )(query_act, key_act, value_act, attn_out, grad_out, pair_bias, log_norm, back_weight)
    column_grad = jnp.transpose(pairs, (2, 0, 1, 3)).reshape(own, n * rows, channels)
    return (column_grad, bias_grad)


def solution(mesh):
    rows = P(("dp", "rows"), None, None)
    return jax.shard_map(
        functools.partial(local, mesh.shape["rows"]),
        mesh=mesh,
        in_specs=(rows, rows, rows, rows, rows, P(None, ("dp", "rows"), None), rows, P()),
        out_specs=(P("rows", "dp", None), P(None, ("dp", "rows"), None)),
        check_vma=False,
    )
```

```python
import functools

import jax
import jax.numpy as jnp
from jax import lax
from jax.experimental import pallas as pl
from jax.experimental.pallas import tpu as pltpu
from jax.sharding import PartitionSpec as P

MESH = pl.DeviceIdType.MESH
BLOCK = 64
UNROLL = 16
F32 = jnp.float32
BF16 = jnp.bfloat16


def repeat(count, body):
    if count <= UNROLL:
        for step in range(count):
            body(step)
    else:
        lax.fori_loop(0, count, lambda step, carry: (body(step), carry)[1], 0)


def block_of(length):
    for width in range(min(length, BLOCK), 0, -1):
        if length % width == 0:
            return width


def nt(left, right):
    return lax.dot_general(left, right, (((1,), (1,)), ((), ())), preferred_element_type=F32)


def tn(left, right):
    return lax.dot_general(left, right, (((0,), (0,)), ((), ())), preferred_element_type=F32)


def nn(left, right):
    return jnp.dot(left, right, preferred_element_type=F32)


def kernel(
    n,
    query_hbm, key_hbm, value_hbm, out_hbm, grad_hbm, bias_hbm, norm_hbm, weight_hbm,
    pair_out, bias_out,
    query, key, value, attn, grad, bias, norm, weight,
    factor_own, factor, part, part_in, probs_free, score_free,
    key_wide, norm_rows, joined, pair_send,
    in_sem, factor_sem, part_sem, pair_sem, own_sem,
):
    me = lax.axis_index("rows")
    rows, length, width = query.shape
    heads = bias.shape[0]
    own = bias.shape[1]
    size = width // heads
    scale = size ** (-0.5)
    block = block_of(length)
    chunks = length // block
    owners = block // own
    wide = heads * length

    loads = []
    for at, (source, target) in enumerate(
        (
            (bias_hbm, bias), (query_hbm, query), (key_hbm, key), (norm_hbm, norm),
            (grad_hbm, grad), (out_hbm, attn), (value_hbm, value), (weight_hbm, weight),
        )
    ):
        load = pltpu.make_async_copy(source, target, in_sem.at[at])
        load.start()
        loads.append(load)

    upper = me * 2 // n
    near = upper * me + (1 - upper) * (n - 1 - me)

    def peer(step):
        other = step + (step - near + n) // n
        return upper * other + (1 - upper) * (n - 1 - other)

    barrier = pltpu.get_barrier_semaphore()
    repeat(
        n - 1,
        lambda step: pl.semaphore_signal(
            barrier, inc=1, device_id={"rows": peer(step)}, device_id_type=MESH
        ),
    )

    loads[0].wait()
    own_factor = jnp.exp(
        jnp.concatenate([bias[h].astype(F32) for h in range(heads)], axis=1)
    )
    factor_own[...] = own_factor
    for load in loads[1:7]:
        load.wait()

    head_mask = (
        lax.broadcasted_iota(jnp.int32, (wide, width), 0) // length
        == lax.broadcasted_iota(jnp.int32, (wide, width), 1) // size
    )
    spread = (
        lax.broadcasted_iota(jnp.int32, (2 * width, wide), 0) % width // size
        == lax.broadcasted_iota(jnp.int32, (2 * width, wide), 1) // length
    ).astype(F32).astype(BF16)
    norm_spread = (
        lax.broadcasted_iota(jnp.int32, (3 * heads, wide), 0) % heads
        == lax.broadcasted_iota(jnp.int32, (3 * heads, wide), 1) // length
    ).astype(F32).astype(BF16)

    def widen(array):
        zero = jnp.zeros((wide, width), BF16)
        return jnp.where(head_mask, jnp.concatenate([array] * heads, axis=0), zero)

    def norm_terms(array):
        first = array.astype(BF16).astype(F32)
        second = (array - first).astype(BF16).astype(F32)
        third = array - first - second
        return jnp.concatenate([first, second, third], axis=0).astype(BF16)

    for i in range(rows):
        key_wide[i] = widen(key[i])
        if chunks > 1:
            same = (
                lax.broadcasted_iota(jnp.int32, (3 * heads, 3 * heads), 0)
                == lax.broadcasted_iota(jnp.int32, (3 * heads, 3 * heads), 1)
            ).astype(F32).astype(BF16)
            norm_rows[i] = tn(norm_terms(norm[i]), same)

    def free_part(chunk):
        at = chunk * block if chunks == 1 else pl.multiple_of(chunk * block, block)
        total = None
        for i in range(rows):
            span = pl.ds(at, block)
            grad_i = grad[i, span, :]
            product = grad_i.astype(F32) * attn[i, span, :].astype(F32)
            high = product.astype(BF16)
            low = (product - high.astype(F32)).astype(BF16)
            delta = nn(jnp.concatenate([high, low], axis=1), spread)
            if chunks == 1:
                norm_wide = tn(norm_terms(norm[i]), norm_spread)
            else:
                norm_wide = nn(norm_rows[i, span, :].astype(BF16), norm_spread)
            scores = nt(query[i, span, :], key_wide[i]) * scale
            probs = jnp.exp(scores - norm_wide)
            score = probs * (nt(grad_i, widen(value[i])) - delta)
            probs_free[i, span, :] = probs
            score_free[i, span, :] = score
            total = score if total is None else total + score
        part[pl.ds(chunk * owners, owners)] = total.reshape(owners, own, wide)

    repeat(chunks, free_part) if chunks == 1 else lax.fori_loop(
        0, chunks, lambda c, carry: (free_part(c), carry)[1], 0
    )
    factor[me] = own_factor

    pl.semaphore_wait(barrier, n - 1)

    def send_factor(step):
        pltpu.make_async_remote_copy(
            src_ref=factor_own, dst_ref=factor.at[me],
            send_sem=factor_sem.at[0], recv_sem=factor_sem.at[1],
            device_id={"rows": peer(step)}, device_id_type=MESH,
        ).start()

    def send_part(step):
        other = peer(step)
        pltpu.make_async_remote_copy(
            src_ref=part.at[other], dst_ref=part_in.at[me],
            send_sem=part_sem.at[0], recv_sem=part_sem.at[1],
            device_id={"rows": other}, device_id_type=MESH,
        ).start()

    def send_pair(step):
        other = peer(step)
        pltpu.make_async_remote_copy(
            src_ref=pair_send.at[other], dst_ref=pair_out.at[me],
            send_sem=pair_sem.at[0], recv_sem=pair_sem.at[1],
            device_id={"rows": other}, device_id_type=MESH,
        ).start()

    def all_of(ref, sem):
        view = ref.at[pl.ds(0, n - 1)]
        pltpu.make_async_copy(view, view, sem).wait()

    repeat(n - 1, send_factor)
    repeat(n - 1, send_part)
    part_in[me] = part[me]
    loads[7].wait()
    all_of(factor, factor_sem.at[1])

    def fold(array):
        folded = None
        for h in range(heads):
            keep = lax.broadcasted_iota(jnp.int32, (length, width), 1) // size == h
            piece = jnp.where(keep, array[h * length : (h + 1) * length], 0.0)
            folded = piece if folded is None else folded + piece
        return folded

    if chunks == 1:
        factor_all = factor[...].reshape(length, wide)
        pieces = []
        for i in range(rows):
            probs_low = (probs_free[i] * factor_all).astype(BF16)
            score_low = (score_free[i] * factor_all).astype(BF16)
            grad_query = nn(score_low, key_wide[i]) * scale
            grad_key = fold(tn(score_low, query[i])) * scale
            grad_value = fold(tn(probs_low, grad[i]))
            pieces.append(
                jnp.concatenate([grad_query, grad_key, grad_value], axis=1).astype(BF16)
            )
        for i in range(rows):
            pair = nn(pieces[i], weight[...]).astype(BF16)
            pair_send[:, i] = pair.reshape(n, own, weight.shape[1])
    else:
        for i in range(rows):
            joined[...] = jnp.zeros_like(joined)

            def advance(chunk, carry):
                span = pl.ds(pl.multiple_of(chunk * block, block), block)
                factor_part = factor[pl.ds(chunk * owners, owners)].reshape(block, wide)
                probs_low = (probs_free[i, span, :] * factor_part).astype(BF16)
                score_low = (score_free[i, span, :] * factor_part).astype(BF16)
                joined[0, span, :] = nn(score_low, key_wide[i]) * scale
                joined[1] += fold(tn(score_low, query[i, span, :]))
                joined[2] += fold(tn(probs_low, grad[i, span, :]))
                return carry

            lax.fori_loop(0, chunks, advance, 0)
            whole = jnp.concatenate(
                [joined[0], joined[1] * scale, joined[2]], axis=1
            ).astype(BF16)
            pair = nn(whole, weight[...]).astype(BF16)
            pair_send[:, i] = pair.reshape(n, own, weight.shape[1])

    keep_own = pltpu.make_async_copy(pair_send.at[me], pair_out.at[me], own_sem)
    keep_own.start()
    repeat(n - 1, send_pair)

    all_of(part_in, part_sem.at[1])
    total = jnp.sum(part_in[...], axis=0) * factor_own[...]
    for h in range(heads):
        bias_out[h] = total[:, h * length : (h + 1) * length]

    keep_own.wait()
    all_of(factor, factor_sem.at[0])
    all_of(part_in, part_sem.at[0])
    all_of(pair_out, pair_sem.at[0])
    all_of(pair_out, pair_sem.at[1])


def local(n, query_act, key_act, value_act, attn_out, grad_out, pair_bias, log_norm, back_weight):
    rows, length, width = query_act.shape
    heads, own, _ = pair_bias.shape
    channels = back_weight.shape[1]
    wide = heads * length
    chunked = length // block_of(length) > 1
    act = pltpu.VMEM((rows, length, width), BF16)
    anywhere = pl.BlockSpec(memory_space=pl.ANY)
    pairs, bias_grad = pl.pallas_call(
        functools.partial(kernel, n),
        out_shape=(
            pltpu.VMEM((n, rows, own, channels), BF16),
            pltpu.VMEM((heads, own, length), F32),
        ),
        in_specs=[anywhere] * 8,
        out_specs=(pl.BlockSpec(memory_space=pltpu.VMEM), pl.BlockSpec(memory_space=pltpu.VMEM)),
        scratch_shapes=[
            act, act, act, act, act,
            pltpu.VMEM(pair_bias.shape, BF16),
            pltpu.VMEM(log_norm.shape, F32),
            pltpu.VMEM(back_weight.shape, BF16),
            pltpu.VMEM((own, wide), F32),
            pltpu.VMEM((n, own, wide), F32),
            pltpu.VMEM((n, own, wide), F32),
            pltpu.VMEM((n, own, wide), F32),
            pltpu.VMEM((rows, length, wide), F32),
            pltpu.VMEM((rows, length, wide), F32),
            pltpu.VMEM((rows, wide, width), BF16),
            pltpu.VMEM((rows, length, 3 * heads) if chunked else (rows, 8, 3 * heads), F32),
            pltpu.VMEM((3, length, width) if chunked else (3, 8, 128), F32),
            pltpu.VMEM((n, rows, own, channels), BF16),
            pltpu.SemaphoreType.DMA((8,)),
            pltpu.SemaphoreType.DMA((2,)),
            pltpu.SemaphoreType.DMA((2,)),
            pltpu.SemaphoreType.DMA((2,)),
            pltpu.SemaphoreType.DMA,
        ],
        compiler_params=pltpu.CompilerParams(
            collective_id=0, has_side_effects=True, vmem_limit_bytes=67043328 - (2 << 20)
        ),
    )(query_act, key_act, value_act, attn_out, grad_out, pair_bias, log_norm, back_weight)
    column_grad = jnp.transpose(pairs, (2, 0, 1, 3)).reshape(own, n * rows, channels)
    return (column_grad, bias_grad)


def solution(mesh):
    rows = P(("dp", "rows"), None, None)
    return jax.shard_map(
        functools.partial(local, mesh.shape["rows"]),
        mesh=mesh,
        in_specs=(rows, rows, rows, rows, rows, P(None, ("dp", "rows"), None), rows, P()),
        out_specs=(P("rows", "dp", None), P(None, ("dp", "rows"), None)),
        check_vma=False,
    )
```

```python
import functools

import jax
import jax.numpy as jnp
from jax import lax
from jax.experimental import pallas as pl
from jax.experimental.pallas import tpu as pltpu
from jax.sharding import PartitionSpec as P

MESH = pl.DeviceIdType.MESH
BLOCK = 64
UNROLL = 16
F32 = jnp.float32
BF16 = jnp.bfloat16


def repeat(count, body):
    if count <= UNROLL:
        for step in range(count):
            body(step)
    else:
        lax.fori_loop(0, count, lambda step, carry: (body(step), carry)[1], 0)


def block_of(length):
    for width in range(min(length, BLOCK), 0, -1):
        if length % width == 0:
            return width


def nt(left, right):
    return lax.dot_general(left, right, (((1,), (1,)), ((), ())), preferred_element_type=F32)


def tn(left, right):
    return lax.dot_general(left, right, (((0,), (0,)), ((), ())), preferred_element_type=F32)


def nn(left, right):
    return jnp.dot(left, right, preferred_element_type=F32)


def kernel(
    n,
    query_hbm, key_hbm, value_hbm, out_hbm, grad_hbm, bias_hbm, norm_hbm, weight_hbm,
    pair_out, bias_out,
    query, key, value, attn, grad, bias, norm, weight,
    factor_own, factor, part, part_in, probs_free, score_free,
    key_wide, norm_rows, joined, pair_send,
    in_sem, factor_sem, part_sem, pair_sem, own_sem,
):
    me = lax.axis_index("rows")
    rows, length, width = query.shape
    heads = bias.shape[0]
    own = bias.shape[1]
    size = width // heads
    scale = size ** (-0.5)
    block = block_of(length)
    chunks = length // block
    owners = block // own
    wide = heads * length

    loads = []
    for at, (source, target) in enumerate(
        (
            (bias_hbm, bias), (query_hbm, query), (key_hbm, key), (norm_hbm, norm),
            (grad_hbm, grad), (out_hbm, attn), (value_hbm, value), (weight_hbm, weight),
        )
    ):
        load = pltpu.make_async_copy(source, target, in_sem.at[at])
        load.start()
        loads.append(load)

    upper = me * 2 // n
    near = upper * me + (1 - upper) * (n - 1 - me)

    def peer(step):
        other = step + (step - near + n) // n
        return upper * other + (1 - upper) * (n - 1 - other)

    barrier = pltpu.get_barrier_semaphore()
    repeat(
        n - 1,
        lambda step: pl.semaphore_signal(
            barrier, inc=1, device_id={"rows": peer(step)}, device_id_type=MESH
        ),
    )

    loads[0].wait()
    own_factor = jnp.exp(
        jnp.concatenate([bias[h].astype(F32) for h in range(heads)], axis=1)
    )
    factor_own[...] = own_factor
    for load in loads[1:7]:
        load.wait()

    head_mask = (
        lax.broadcasted_iota(jnp.int32, (wide, width), 0) // length
        == lax.broadcasted_iota(jnp.int32, (wide, width), 1) // size
    )
    spread = (
        lax.broadcasted_iota(jnp.int32, (2 * width, wide), 0) % width // size
        == lax.broadcasted_iota(jnp.int32, (2 * width, wide), 1) // length
    ).astype(F32).astype(BF16)
    norm_spread = (
        lax.broadcasted_iota(jnp.int32, (3 * heads, wide), 0) % heads
        == lax.broadcasted_iota(jnp.int32, (3 * heads, wide), 1) // length
    ).astype(F32).astype(BF16)

    def widen(array):
        zero = jnp.zeros((wide, width), BF16)
        return jnp.where(head_mask, jnp.concatenate([array] * heads, axis=0), zero)

    def norm_terms(array):
        first = array.astype(BF16).astype(F32)
        second = (array - first).astype(BF16).astype(F32)
        third = array - first - second
        return jnp.concatenate([first, second, third], axis=0).astype(BF16)

    for i in range(rows):
        key_wide[i] = widen(key[i])
        if chunks > 1:
            same = (
                lax.broadcasted_iota(jnp.int32, (3 * heads, 3 * heads), 0)
                == lax.broadcasted_iota(jnp.int32, (3 * heads, 3 * heads), 1)
            ).astype(F32).astype(BF16)
            norm_rows[i] = tn(norm_terms(norm[i]), same)

    def free_part(chunk):
        at = chunk * block if chunks == 1 else pl.multiple_of(chunk * block, block)
        total = None
        for i in range(rows):
            span = pl.ds(at, block)
            grad_i = grad[i, span, :]
            product = grad_i.astype(F32) * attn[i, span, :].astype(F32)
            high = product.astype(BF16)
            low = (product - high.astype(F32)).astype(BF16)
            delta = nn(jnp.concatenate([high, low], axis=1), spread)
            if chunks == 1:
                norm_wide = tn(norm_terms(norm[i]), norm_spread)
            else:
                norm_wide = nn(norm_rows[i, span, :].astype(BF16), norm_spread)
            scores = nt(query[i, span, :], key_wide[i]) * scale
            probs = jnp.exp(scores - norm_wide)
            score = probs * (nt(grad_i, widen(value[i])) - delta)
            probs_free[i, span, :] = probs
            score_free[i, span, :] = score
            total = score if total is None else total + score
        part[pl.ds(chunk * owners, owners)] = total.reshape(owners, own, wide)

    repeat(chunks, free_part) if chunks == 1 else lax.fori_loop(
        0, chunks, lambda c, carry: (free_part(c), carry)[1], 0
    )
    factor[me] = own_factor

    pl.semaphore_wait(barrier, n - 1)

    def send_factor(step):
        pltpu.make_async_remote_copy(
            src_ref=factor_own, dst_ref=factor.at[me],
            send_sem=factor_sem.at[0], recv_sem=factor_sem.at[1],
            device_id={"rows": peer(step)}, device_id_type=MESH,
        ).start()

    def send_part(step):
        other = peer(step)
        pltpu.make_async_remote_copy(
            src_ref=part.at[other], dst_ref=part_in.at[me],
            send_sem=part_sem.at[0], recv_sem=part_sem.at[1],
            device_id={"rows": other}, device_id_type=MESH,
        ).start()

    def send_pair(step):
        other = peer(step)
        pltpu.make_async_remote_copy(
            src_ref=pair_send.at[other], dst_ref=pair_out.at[me],
            send_sem=pair_sem.at[0], recv_sem=pair_sem.at[1],
            device_id={"rows": other}, device_id_type=MESH,
        ).start()

    def all_of(ref, sem):
        view = ref.at[pl.ds(0, n - 1)]
        pltpu.make_async_copy(view, view, sem).wait()

    repeat(n - 1, send_factor)
    repeat(n - 1, send_part)
    part_in[me] = part[me]
    loads[7].wait()
    all_of(factor, factor_sem.at[1])

    def fold(array):
        folded = None
        for h in range(heads):
            keep = lax.broadcasted_iota(jnp.int32, (length, width), 1) // size == h
            piece = jnp.where(keep, array[h * length : (h + 1) * length], 0.0)
            folded = piece if folded is None else folded + piece
        return folded

    if chunks == 1:
        factor_all = factor[...].reshape(length, wide)
        pieces = []
        for i in range(rows):
            probs_low = (probs_free[i] * factor_all).astype(BF16)
            score_low = (score_free[i] * factor_all).astype(BF16)
            grad_query = nn(score_low, key_wide[i]) * scale
            grad_key = fold(tn(score_low, query[i])) * scale
            grad_value = fold(tn(probs_low, grad[i]))
            pieces.append(
                jnp.concatenate([grad_query, grad_key, grad_value], axis=1).astype(BF16)
            )
        for i in range(rows):
            pair = nn(pieces[i], weight[...]).astype(BF16)
            pair_send[:, i] = pair.reshape(n, own, weight.shape[1])
    else:
        for i in range(rows):
            joined[...] = jnp.zeros_like(joined)

            def advance(chunk, carry):
                span = pl.ds(pl.multiple_of(chunk * block, block), block)
                factor_part = factor[pl.ds(chunk * owners, owners)].reshape(block, wide)
                probs_low = (probs_free[i, span, :] * factor_part).astype(BF16)
                score_low = (score_free[i, span, :] * factor_part).astype(BF16)
                joined[0, span, :] = nn(score_low, key_wide[i]) * scale
                joined[1] += fold(tn(score_low, query[i, span, :]))
                joined[2] += fold(tn(probs_low, grad[i, span, :]))
                return carry

            lax.fori_loop(0, chunks, advance, 0)
            whole = jnp.concatenate(
                [joined[0], joined[1] * scale, joined[2]], axis=1
            ).astype(BF16)
            pair = nn(whole, weight[...]).astype(BF16)
            pair_send[:, i] = pair.reshape(n, own, weight.shape[1])

    keep_own = pltpu.make_async_copy(pair_send.at[me], pair_out.at[me], own_sem)
    keep_own.start()
    repeat(n - 1, send_pair)

    all_of(part_in, part_sem.at[1])
    total = jnp.sum(part_in[...], axis=0) * factor_own[...]
    bias_out[...] = total

    keep_own.wait()
    all_of(factor, factor_sem.at[0])
    all_of(part_in, part_sem.at[0])
    all_of(pair_out, pair_sem.at[0])
    all_of(pair_out, pair_sem.at[1])


def finish(pairs, total, column_out, bias_out):
    n, rows, own, channels = pairs.shape
    heads, _, length = bias_out.shape
    landed = pairs[...].astype(F32).reshape(n * rows, own, channels)
    column_out[...] = jnp.transpose(landed, (1, 0, 2)).astype(BF16)
    for h in range(heads):
        bias_out[h] = total[:, h * length : (h + 1) * length]


def local(n, query_act, key_act, value_act, attn_out, grad_out, pair_bias, log_norm, back_weight):
    rows, length, width = query_act.shape
    heads, own, _ = pair_bias.shape
    channels = back_weight.shape[1]
    wide = heads * length
    chunked = length // block_of(length) > 1
    act = pltpu.VMEM((rows, length, width), BF16)
    anywhere = pl.BlockSpec(memory_space=pl.ANY)
    pairs, bias_grad = pl.pallas_call(
        functools.partial(kernel, n),
        out_shape=(
            pltpu.VMEM((n, rows, own, channels), BF16),
            pltpu.VMEM((own, wide), F32),
        ),
        in_specs=[anywhere] * 8,
        out_specs=(pl.BlockSpec(memory_space=pltpu.VMEM), pl.BlockSpec(memory_space=pltpu.VMEM)),
        scratch_shapes=[
            act, act, act, act, act,
            pltpu.VMEM(pair_bias.shape, BF16),
            pltpu.VMEM(log_norm.shape, F32),
            pltpu.VMEM(back_weight.shape, BF16),
            pltpu.VMEM((own, wide), F32),
            pltpu.VMEM((n, own, wide), F32),
            pltpu.VMEM((n, own, wide), F32),
            pltpu.VMEM((n, own, wide), F32),
            pltpu.VMEM((rows, length, wide), F32),
            pltpu.VMEM((rows, length, wide), F32),
            pltpu.VMEM((rows, wide, width), BF16),
            pltpu.VMEM((rows, length, 3 * heads) if chunked else (rows, 8, 3 * heads), F32),
            pltpu.VMEM((3, length, width) if chunked else (3, 8, 128), F32),
            pltpu.VMEM((n, rows, own, channels), BF16),
            pltpu.SemaphoreType.DMA((8,)),
            pltpu.SemaphoreType.DMA((2,)),
            pltpu.SemaphoreType.DMA((2,)),
            pltpu.SemaphoreType.DMA((2,)),
            pltpu.SemaphoreType.DMA,
        ],
        compiler_params=pltpu.CompilerParams(
            collective_id=0, has_side_effects=True, vmem_limit_bytes=67043328 - (2 << 20)
        ),
    )(query_act, key_act, value_act, attn_out, grad_out, pair_bias, log_norm, back_weight)
    vmem = pl.BlockSpec(memory_space=pltpu.VMEM)
    return pl.pallas_call(
        finish,
        out_shape=(
            jax.ShapeDtypeStruct((own, n * rows, channels), BF16),
            jax.ShapeDtypeStruct((heads, own, length), F32),
        ),
        in_specs=[vmem, vmem],
        out_specs=(vmem, vmem),
    )(
        pltpu.with_memory_space_constraint(pairs, pltpu.VMEM),
        pltpu.with_memory_space_constraint(bias_grad, pltpu.VMEM),
    )


def solution(mesh):
    rows = P(("dp", "rows"), None, None)
    return jax.shard_map(
        functools.partial(local, mesh.shape["rows"]),
        mesh=mesh,
        in_specs=(rows, rows, rows, rows, rows, P(None, ("dp", "rows"), None), rows, P()),
        out_specs=(P("rows", "dp", None), P(None, ("dp", "rows"), None)),
        check_vma=False,
    )
```
